32 devices in a mesh: groups: 2 (over y), ctx: 4 (over x, core), tp: 4 (over z).
Axes of the slice: x: 2, y: 2, z: 4, core: 2. Of those that a mesh axis runs over, the one named last changes fastest.
Arguments:
- tokens: bfloat16 [2048, 4096], P(('groups', 'ctx', 'tp')), parts along dimension 0, may hold values from -6 to 6
- gate_weight: bfloat16 [4096, 8192], P(None, 'tp'), may hold values from -0.09375 to 0.09375
- value_weight: bfloat16 [4096, 8192], P(None, 'tp'), may hold values from -0.09375 to 0.09375
- key_weight: bfloat16 [4096, 1024], P(None, 'tp'), may hold values from -0.09375 to 0.09375
- query_weight: bfloat16 [4096, 1024], P(None, 'tp'), may hold values from -0.09375 to 0.09375
- step_weight: bfloat16 [4096, 128], P(None, 'tp'), may hold values from -0.09375 to 0.09375
- value_conv: float32 [4, 8192], P(None, 'tp'), may hold values from -3 to 3
- key_conv: float32 [4, 1024], P(None, 'tp'), may hold values from -3 to 3
- query_conv: float32 [4, 1024], P(None, 'tp'), may hold values from -3 to 3
- step_bias: float32 [128], P('tp'), may hold values from -3 to -1
- decay_log: float32 [128], P('tp'), may hold values from -6.5 to -1.5
- skip_gain: float32 [128], P('tp'), may hold values from 0.5 to 1.5
- norm_gain: float32 [8192], P('tp'), may hold values from 0.1 to 1.9
- out_weight: bfloat16 [8192, 4096], P('tp'), may hold values from -0.0625 to 0.0625
Outputs:
- layer_out: bfloat16 [2048, 4096], P(('groups', 'ctx', 'tp')), parts along dimension 0
The draws below stay inside these ranges and needn't reach their ends.
There are 2 independent parts, one for each index of `groups`. The reference program is written for one: setup_inputs(seed, part) draws one part's arguments, and reference() takes and returns one part's arrays. A program takes and returns all parts, laid end to end along the dimension named above; an argument that names none is the same for every part. Nothing has to cross between parts.
All inputs are finite; a program needn't handle non-finite values.
Results may differ from the reference program's by a relative error of at most 0.024.
Values may be sent and summed in bfloat16 or wider, within the bound.
No kernel may reach another device: no remote copies, remote signals or barrier semaphores. Data moves between devices by JAX's collectives and lax.ppermute only.
A program may use at most 192 MiB of HBM per device.

```python
import jax
import jax.numpy as jnp
from jax import lax

D = 4096
HEADS = 128
HEAD_DIM = 64
STATE = 128
GROUPS = 8
CONV = 4
INNER = 8192
BLOCK = 128
SEQ = 1024
N_TP = 4


def block_levels(key, shape, cuts, least, top_value):
    def one(dim, parts):
        draws = jax.random.uniform(jax.random.fold_in(jax.random.fold_in(key, 6), dim), (parts,), jnp.float32, least / len(cuts), top_value / len(cuts))
        return jnp.repeat(jnp.exp(draws), shape[dim] // parts).reshape((-1,) + (1,) * (len(shape) - dim - 1))

    gain = one(*cuts[0])
    for cut in cuts[1:]:
        gain = gain * one(*cut)
    return gain


def normal_values(stream_key, extent, spread, most, shards=(), held_as=jnp.bfloat16):
    loudness = block_levels(stream_key, extent, shards, -0.22, 0.18) if shards else 1.0
    entries = jax.random.normal(stream_key, extent, jnp.float32) * spread * loudness
    return jnp.minimum(jnp.maximum(entries, -most), most).astype(held_as)


def setup_inputs(seed: int = 0, part: int = 0) -> dict:
    streams_of = jax.random.split(jax.random.key(seed), 15)
    own_keys = jax.random.split(jax.random.fold_in(streams_of[14], part), 15)
    return {
        "tokens": normal_values(own_keys[0], (SEQ, D), 1.0, 6.0, ((0, 16),)),
        "gate_weight": normal_values(streams_of[1], (D, INNER), D ** -0.5, 0.09375, ((1, 4),)),
        "value_weight": normal_values(streams_of[2], (D, INNER), D ** -0.5, 0.09375, ((1, 4),)),
        "key_weight": normal_values(streams_of[3], (D, GROUPS * STATE), D ** -0.5, 0.09375, ((1, 4),)),
        "query_weight": normal_values(streams_of[4], (D, GROUPS * STATE), D ** -0.5, 0.09375, ((1, 4),)),
        "step_weight": normal_values(streams_of[5], (D, HEADS), D ** -0.5, 0.09375, ((1, 4),)),
        "value_conv": normal_values(streams_of[6], (CONV, INNER), CONV ** -0.5, 3.0, ((1, 4),), jnp.float32),
        "key_conv": normal_values(streams_of[7], (CONV, GROUPS * STATE), CONV ** -0.5, 3.0, ((1, 4),), jnp.float32),
        "query_conv": normal_values(streams_of[8], (CONV, GROUPS * STATE), CONV ** -0.5, 3.0, ((1, 4),), jnp.float32),
        "step_bias": jnp.clip(-3.0 + 2.0 * jax.random.uniform(streams_of[9], (HEADS,), jnp.float32) ** block_levels(streams_of[9], (HEADS,), ((0, 4),), -0.2, 0.2), -3.0, -1.0),
        "decay_log": jnp.clip(-6.5 + 5.0 * jax.random.uniform(streams_of[10], (HEADS,), jnp.float32) ** block_levels(streams_of[10], (HEADS,), ((0, 4),), -0.2, 0.2), -6.5, -1.5),
        "skip_gain": jnp.clip(0.5 + 1.0 * jax.random.uniform(streams_of[11], (HEADS,), jnp.float32) ** block_levels(streams_of[11], (HEADS,), ((0, 4),), -0.2, 0.2), 0.5, 1.5),
        "norm_gain": jnp.clip(1.0 + 0.18 * jax.random.normal(streams_of[12], (INNER,), jnp.float32), 0.1, 1.9),
        "out_weight": normal_values(streams_of[13], (INNER, D), INNER ** -0.5, 0.0625, ((0, 4),)),
    }


def causal_mix(padded, kernel, length):
    total = padded[0:length] * kernel[0]
    for tap_index in range(1, kernel.shape[0]):
        total = total + padded[tap_index:tap_index + length] * kernel[tap_index]
    return total

def convolve(pre, kernel):
    padded = jnp.pad(pre.astype(jnp.float32), ((CONV - 1, 0), (0, 0)))
    return jax.nn.silu(causal_mix(padded, kernel, SEQ)).astype(jnp.bfloat16)

def reference(tokens, gate_weight, value_weight, key_weight, query_weight, step_weight, value_conv, key_conv, query_conv, step_bias, decay_log, skip_gain, norm_gain, out_weight):
    gate_in = jnp.dot(tokens, gate_weight, preferred_element_type=jnp.float32).astype(jnp.bfloat16)
    value_pre = jnp.dot(tokens, value_weight, preferred_element_type=jnp.float32).astype(jnp.bfloat16)
    key_pre = jnp.dot(tokens, key_weight, preferred_element_type=jnp.float32).astype(jnp.bfloat16)
    query_pre = jnp.dot(tokens, query_weight, preferred_element_type=jnp.float32).astype(jnp.bfloat16)
    step_raw = jnp.dot(tokens, step_weight, preferred_element_type=jnp.float32)
    value_act = convolve(value_pre, value_conv)
    key_act = convolve(key_pre, key_conv)
    query_act = convolve(query_pre, query_conv)
    step = jax.nn.softplus(step_raw + step_bias)
    rate = -jnp.exp(decay_log) * step
    block_count = SEQ // BLOCK
    per_group = HEADS // GROUPS
    cum = jnp.cumsum(rate.reshape(block_count, BLOCK, HEADS), axis=1)
    steps_blk = step.reshape(block_count, BLOCK, HEADS)
    values = value_act.reshape(block_count, BLOCK, HEADS, HEAD_DIM)
    keys = key_act.reshape(block_count, BLOCK, GROUPS, STATE)
    queries = query_act.reshape(block_count, BLOCK, GROUPS, STATE)
    causal = jnp.tril(jnp.ones((BLOCK, BLOCK), jnp.bool_))

    def one_block(carry, item):
        cum_b, step_b, value_b, key_b, query_b = item
        scores = jnp.einsum('tgn,ugn->gtu', query_b.astype(jnp.float32), key_b.astype(jnp.float32))
        scores = jnp.repeat(scores, per_group, axis=0)
        cum_t = cum_b.T
        diff = cum_t[:, :, None] - cum_t[:, None, :]
        factor = jnp.where(causal, jnp.exp(jnp.where(causal, diff, 0.0)), 0.0)
        weights = (scores * factor * step_b.T[:, None, :]).astype(jnp.bfloat16)
        inner = jnp.einsum('htu,uhp->thp', weights.astype(jnp.float32), value_b.astype(jnp.float32))
        tail = jnp.exp(cum_b[-1:] - cum_b) * step_b
        weighted = (value_b.astype(jnp.float32) * tail[:, :, None]).astype(jnp.bfloat16)
        key_heads = jnp.repeat(key_b, per_group, axis=1)
        query_heads = jnp.repeat(query_b, per_group, axis=1)
        outer = jnp.einsum('thn,hnp->thp', query_heads.astype(jnp.float32), carry, precision=lax.Precision.HIGHEST)
        result = inner + jnp.exp(cum_b)[:, :, None] * outer + skip_gain[:, None] * value_b.astype(jnp.float32)
        local = jnp.einsum('uhn,uhp->hnp', key_heads.astype(jnp.float32), weighted.astype(jnp.float32))
        carry = jnp.exp(cum_b[-1])[:, None, None] * carry + local
        return (carry, result)
    start = jnp.zeros((HEADS, STATE, HEAD_DIM), jnp.float32)
    _, results = lax.scan(one_block, start, (cum, steps_blk, values, keys, queries))
    ssm_out = results.reshape(SEQ, INNER)
    gated = ssm_out * jax.nn.silu(gate_in.astype(jnp.float32))
    span = INNER // GROUPS
    grouped = gated.reshape(SEQ, GROUPS, span)
    scale = lax.rsqrt(lax.optimization_barrier(jnp.mean(grouped * grouped, axis=2)) + 1e-05)
    normed = ((grouped * scale[:, :, None]).reshape(SEQ, INNER) * norm_gain).astype(jnp.bfloat16)
    block_width = INNER // N_TP

    def add_block(total, block_index):
        first = (block_index * block_width).astype(jnp.int32)
        cols = lax.dynamic_slice_in_dim(normed, first, block_width, 1)
        rows = lax.dynamic_slice_in_dim(out_weight, first, block_width, 0)
        part = jnp.dot(cols, rows, preferred_element_type=jnp.float32).astype(jnp.bfloat16)
        part = lax.optimization_barrier(part)
        return (total + part.astype(jnp.float32), None)
    summed, _ = lax.scan(add_block, jnp.zeros((SEQ, D), jnp.float32), jnp.arange(N_TP, dtype=jnp.int32))
    return summed.astype(jnp.bfloat16)
```

```python
import jax
import jax.numpy as jnp
from jax import lax
from jax.experimental import pallas as pl
from jax.experimental.pallas import tpu as pltpu
from jax.sharding import PartitionSpec as P

STATE = 128
GROUPS = 8
INNER = 8192


def passed_along(shard, axis, by):
    count = lax.axis_size(axis)
    pairs = [(i, i + by) for i in range(count) if 0 <= i + by < count]
    return lax.ppermute(shard, axis, pairs)


def from_partner(block, axis, distance):
    count = lax.axis_size(axis)
    route = []
    for low in range(count):
        high = low | 1 << distance
        if high != low and high < count:
            route += [(low, high), (high, low)]
    return lax.ppermute(block, axis, route)


def causal_mix(padded, kernel, length):
    total = padded[0:length] * kernel[0]
    for tap_index in range(1, kernel.shape[0]):
        total = total + padded[tap_index : tap_index + length] * kernel[tap_index]
    return total


def general_shards(
    tokens,
    gate_weight,
    value_weight,
    key_weight,
    query_weight,
    step_weight,
    value_conv,
    key_conv,
    query_conv,
    step_bias,
    decay_log,
    skip_gain,
    norm_gain,
    out_weight,
):
    tok_dev = tokens.shape[0]
    slab_rows = tok_dev * lax.axis_size("tp")
    columns = gate_weight.shape[1]
    key_cols = key_weight.shape[1]
    heads_here = step_weight.shape[1]
    head_width = columns // heads_here
    block_len = min(128, slab_rows)
    block_count = slab_rows // block_len
    kernel_len = value_conv.shape[0]
    joined = jnp.concatenate(
        [gate_weight, value_weight, key_weight, query_weight, step_weight], axis=1
    )
    projected = jnp.dot(
        lax.all_gather(tokens, "tp", axis=0, tiled=True), joined, preferred_element_type=jnp.float32
    )
    gate_in = projected[:, :columns].astype(jnp.bfloat16)
    mixed_pre = projected[:, columns : 2 * columns + 2 * key_cols].astype(jnp.bfloat16)
    step_raw = projected[:, 2 * columns + 2 * key_cols :]
    border = passed_along(mixed_pre[slab_rows - (kernel_len - 1) :], "ctx", 1)
    padded = jnp.concatenate([border, mixed_pre], axis=0).astype(jnp.float32)
    kernel = jnp.concatenate([value_conv, key_conv, query_conv], axis=1)
    activated = jax.nn.silu(causal_mix(padded, kernel, slab_rows)).astype(jnp.bfloat16)
    value_act = activated[:, :columns]
    key_act = activated[:, columns : columns + key_cols]
    query_act = activated[:, columns + key_cols :]
    group_cols = max(key_cols, STATE)
    reach = group_cols // key_cols
    key_group, query_group = (key_act, query_act)
    for bit_index in range(reach.bit_length() - 1):
        other_keys, other_queries = from_partner((key_group, query_group), "tp", bit_index)
        upper = lax.axis_index("tp") // (1 << bit_index) % 2 == 1
        key_group = jnp.where(
            upper,
            jnp.concatenate([other_keys, key_group], 1),
            jnp.concatenate([key_group, other_keys], 1),
        )
        query_group = jnp.where(
            upper,
            jnp.concatenate([other_queries, query_group], 1),
            jnp.concatenate([query_group, other_queries], 1),
        )
    local_groups = group_cols // STATE
    per_group = heads_here // local_groups
    step = jax.nn.softplus(step_raw + step_bias)
    rate = -jnp.exp(decay_log) * step
    cum = jnp.cumsum(rate.reshape(block_count, block_len, heads_here), axis=1)
    step_blk = step.reshape(block_count, block_len, heads_here)
    values = value_act.reshape(block_count, block_len, heads_here, head_width)
    keys = key_group.reshape(block_count, block_len, local_groups, STATE)
    queries = query_group.reshape(block_count, block_len, local_groups, STATE)
    scores = jnp.einsum("btgn,bugn->gbtu", queries, keys, preferred_element_type=jnp.float32)
    scores = jnp.repeat(scores, per_group, axis=0)
    cum_t = jnp.transpose(cum, (2, 0, 1))
    step_t = jnp.transpose(step_blk, (2, 0, 1))
    causal = jnp.tril(jnp.ones((block_len, block_len), jnp.bool_))
    diff = cum_t[:, :, :, None] - cum_t[:, :, None, :]
    factor = jnp.where(causal, jnp.exp(jnp.where(causal, diff, 0.0)), 0.0)
    weights = (scores * factor * step_t[:, :, None, :]).astype(jnp.bfloat16)
    inner = jnp.einsum("hbtu,buhp->bthp", weights, values, preferred_element_type=jnp.float32)
    tail = jnp.exp(cum[:, -1:, :] - cum) * step_blk
    weighted = (values * tail[:, :, :, None]).astype(jnp.bfloat16)
    key_heads = jnp.repeat(keys, per_group, axis=2)
    query_heads = jnp.repeat(queries, per_group, axis=2)
    local = jnp.einsum("buhn,buhp->bhnp", key_heads, weighted, preferred_element_type=jnp.float32)
    falloff = jnp.exp(cum[:, -1, :])

    def advance(carry, item):
        fade, added = item
        return (fade[:, None, None] * carry + added, carry)

    zero_state = jnp.zeros((heads_here, STATE, head_width), jnp.float32)
    slab_state, _ = lax.scan(advance, zero_state, (falloff, local))
    slab_fall = jnp.exp(jnp.sum(cum[:, -1, :], axis=0))
    inflow = zero_state
    for turn in range(lax.axis_size("ctx") - 1):
        inflow = passed_along(
            (slab_fall[:, None, None] * inflow + slab_state).astype(jnp.bfloat16), "ctx", 1
        ).astype(jnp.float32)
    _, starts = lax.scan(advance, inflow, (falloff, local))
    outer = jnp.einsum(
        "bthn,bhnp->bthp", query_heads.astype(jnp.float32), starts, precision=lax.Precision.HIGHEST
    )
    ssm_out = (
        inner
        + jnp.exp(cum)[:, :, :, None] * outer
        + skip_gain[:, None] * values.astype(jnp.float32)
    )
    ssm_out = ssm_out.reshape(slab_rows, columns)
    gated = ssm_out * jax.nn.silu(gate_in.astype(jnp.float32))
    span = INNER // GROUPS
    piece_len = min(columns, span)
    norm_here = columns // piece_len
    squares = jnp.sum((gated * gated).reshape(slab_rows, norm_here, piece_len), axis=2)
    norm_reach = span // piece_len
    for bit_index in range(norm_reach.bit_length() - 1):
        squares = squares + from_partner(squares, "tp", bit_index)
    scale = lax.rsqrt(squares / span + 1e-05)
    normed = (gated.reshape(slab_rows, norm_here, piece_len) * scale[:, :, None]).reshape(
        slab_rows, columns
    ) * norm_gain
    normed = normed.astype(jnp.bfloat16)
    return lax.psum_scatter(
        jnp.dot(normed, out_weight, preferred_element_type=jnp.float32).astype(jnp.bfloat16),
        "tp",
        scatter_dimension=0,
        tiled=True,
    )


HALO = 16
BLOCK = 128
LANES = 128
F32 = jnp.float32
BF16 = jnp.bfloat16


def cost(flops, moved):
    return pl.CostEstimate(flops=int(flops), bytes_accessed=int(moved), transcendentals=0)


def project(place, pieces, jobs, chunk, depth):
    rows = HALO + 4 * 64
    starts, total = [], 0
    for job in jobs:
        starts.append(total)
        total += job["weight"].shape[1] // job["tile"]

    def spec(shape, at, count, row):
        return pl.BlockSpec(shape, lambda j, _: (row, jnp.clip(j - at, 0, count - 1)))

    in_specs = [
        pl.BlockSpec((64, depth), lambda j, _: (0, chunk)),
        *[pl.BlockSpec((64, depth), lambda j, _: (0, 0))] * 4,
        pl.BlockSpec((8, depth), lambda j, _: (0, chunk)),
    ]
    operands, out_specs, out_shapes = list(pieces), [], []
    for job, at in zip(jobs, starts):
        count = job["weight"].shape[1] // job["tile"]
        in_specs.append(spec((depth, job["tile"]), at, count, chunk))
        operands.append(job["weight"])
        height = rows if job["halo"] else rows - HALO
        if job["partial"] is not None:
            in_specs.append(spec((height, job["tile"]), at, count, 0))
            operands.append(job["partial"])
        if job["grouped"]:
            groups = job["weight"].shape[1] // 16
            out_specs.append(pl.BlockSpec((groups, rows, LANES), lambda j, _: (0, 0, 0)))
            out_shapes.append(jax.ShapeDtypeStruct((groups, rows, LANES), F32))
        else:
            out_specs.append(spec((height, job["tile"]), at, count, 0))
            out_shapes.append(jax.ShapeDtypeStruct((height, job["weight"].shape[1]), job["out"]))

    def kernel(place_ref, own, right1, left1, rot2, last, halo, *refs):
        inputs = list(refs[: len(operands) - 6])
        outputs = list(refs[len(operands) - 6 : -1])
        x = refs[-1]
        j = pl.program_id(0)
        tp = place_ref[0]

        @pl.when(j == 0)
        def _():
            x[0:8, :] = jnp.zeros((8, depth), BF16)
            x[8:16, :] = halo[...]

            def put(distance, block):
                row = pl.multiple_of(HALO + (tp + 4 - distance) % 4 * 64, 16)
                x[pl.ds(row, 64), :] = block

            put(0, own[...])
            put(1, jnp.where(tp == 0, last[...], right1[...]))
            put(2, rot2[...])
            put(3, jnp.where(tp == 3, last[...], left1[...]))

        for job, at in zip(jobs, starts):
            count = job["weight"].shape[1] // job["tile"]
            weight = inputs.pop(0)
            partial = inputs.pop(0) if job["partial"] is not None else None
            out = outputs.pop(0)

            @pl.when((j >= at) & (j < at + count))
            def _(job=job, weight=weight, partial=partial, out=out):
                rows_in = x[...] if job["halo"] else x[HALO:, :]
                result = jnp.dot(rows_in, weight[...], preferred_element_type=F32)
                if partial is not None:
                    result = result + partial[...]
                if job["grouped"]:
                    out[...] = jnp.zeros(out.shape, F32)
                    for group in range(out.shape[0]):
                        out[group, :, 0:16] = result[:, group * 16 : group * 16 + 16]
                else:
                    out[...] = result.astype(out.dtype)

    columns = sum(job["weight"].shape[1] for job in jobs)
    return pl.pallas_call(
        kernel,
        grid_spec=pltpu.PrefetchScalarGridSpec(
            num_scalar_prefetch=1,
            grid=(total,),
            in_specs=in_specs,
            out_specs=out_specs,
            scratch_shapes=[pltpu.VMEM((rows, depth), BF16)],
        ),
        out_shape=out_shapes,
        cost_estimate=cost(2 * rows * depth * columns, 2 * depth * columns + 6 * rows * columns),
        compiler_params=pltpu.CompilerParams(vmem_limit_bytes=40 << 20),
        name="project",
    )(place, *operands)


def silu(v):
    return v / (1.0 + jnp.exp(-v))


def convolved(pre_ref, taps_ref, at, lanes):
    window = pre_ref[at : at + HALO + BLOCK, lanes].astype(F32)
    total = window * taps_ref[3:4, lanes]
    for back in (1, 2, 3):
        total = total + pltpu.roll(window, back, 0) * taps_ref[3 - back : 4 - back, lanes]
    return silu(total[HALO:, :])


def pair_lanes(left, right, low):
    return jnp.where(low, left, right)


def states_kernel(vpre, kpre, vtaps, ktaps, raw, bias, decay, values, keys, cum, cum_t, step_t, local0, slab, fall0, fall):
    tri = jnp.where(
        lax.broadcasted_iota(jnp.int32, (BLOCK, BLOCK), 0) >= lax.broadcasted_iota(jnp.int32, (BLOCK, BLOCK), 1),
        1.0,
        0.0,
    )
    low = lax.broadcasted_iota(jnp.int32, (BLOCK, LANES), 1) < 64
    low1 = low[0:1, :]
    sums, tails = [], []
    for b in range(2):
        rows = slice(b * BLOCK, (b + 1) * BLOCK)
        shifted = raw[0, HALO + b * BLOCK : HALO + (b + 1) * BLOCK, :] + bias[0]
        step = jnp.maximum(shifted, 0.0) + jnp.log1p(jnp.exp(-jnp.abs(shifted)))
        rate = -jnp.exp(decay[0]) * step
        total = jnp.dot(tri, rate, precision=lax.Precision.HIGHEST, preferred_element_type=F32)
        cum[0, rows, :] = total
        cum_t[0, :, rows] = total.T
        step_t[0, :, rows] = step.T
        tails.append(jnp.exp(total[BLOCK - 1 :, :] - total) * step)
        sums.append(total[BLOCK - 1 :, :])
        keys[rows, :] = convolved(kpre, ktaps, b * BLOCK, slice(0, LANES)).astype(BF16)
    both = sums[0] + sums[1]
    for pair in range(8):
        lanes = slice(pair * LANES, (pair + 1) * LANES)
        kept = []
        for b in range(2):
            rows = slice(b * BLOCK, (b + 1) * BLOCK)
            act = convolved(vpre, vtaps, b * BLOCK, lanes).astype(BF16)
            values[rows, lanes] = act
            tail = pair_lanes(tails[b][:, 2 * pair : 2 * pair + 1], tails[b][:, 2 * pair + 1 : 2 * pair + 2], low)
            weighted = (act.astype(F32) * tail).astype(BF16)
            kept.append(
                lax.dot_general(keys[rows, :], weighted, (((0,), (0,)), ((), ())), preferred_element_type=F32)
            )
        spread = [
            jnp.exp(pair_lanes(s[:, 2 * pair : 2 * pair + 1], s[:, 2 * pair + 1 : 2 * pair + 2], low1))
            for s in (sums[0], sums[1], both)
        ]
        local0[:, lanes] = kept[0]
        slab[:, lanes] = (spread[1] * kept[0] + kept[1]).astype(BF16)
        fall0[:, lanes] = spread[0]
        fall[:, lanes] = spread[2]


def states(vpre, kpre, vtaps, ktaps, raw, bias, decay):
    groups = raw.shape[0]
    rows = vpre.shape[0]
    slab_rows = rows - HALO
    wide = 1024
    col = lambda g: (0, g)
    lead = lambda g: (g, 0, 0)
    full = lambda shape, dtype: jax.ShapeDtypeStruct(shape, dtype)
    return pl.pallas_call(
        states_kernel,
        grid=(groups,),
        in_specs=[
            pl.BlockSpec((rows, wide), col),
            pl.BlockSpec((rows, STATE), col),
            pl.BlockSpec((4, wide), col),
            pl.BlockSpec((4, STATE), col),
            pl.BlockSpec((1, rows, LANES), lead),
            pl.BlockSpec((1, 1, LANES), lead),
            pl.BlockSpec((1, 1, LANES), lead),
        ],
        out_specs=[
            pl.BlockSpec((slab_rows, wide), col),
            pl.BlockSpec((slab_rows, STATE), col),
            pl.BlockSpec((1, slab_rows, LANES), lead),
            pl.BlockSpec((1, LANES, slab_rows), lead),
            pl.BlockSpec((1, LANES, slab_rows), lead),
            pl.BlockSpec((STATE, wide), col),
            pl.BlockSpec((STATE, wide), col),
            pl.BlockSpec((1, wide), col),
            pl.BlockSpec((1, wide), col),
        ],
        out_shape=[
            full((slab_rows, groups * wide), BF16),
            full((slab_rows, groups * STATE), BF16),
            full((groups, slab_rows, LANES), F32),
            full((groups, LANES, slab_rows), F32),
            full((groups, LANES, slab_rows), F32),
            full((STATE, groups * wide), F32),
            full((STATE, groups * wide), BF16),
            full((1, groups * wide), F32),
            full((1, groups * wide), F32),
        ],
        cost_estimate=cost(groups * 3e8, groups * 3e6),
        compiler_params=pltpu.CompilerParams(vmem_limit_bytes=32 << 20),
        name="states",
    )(vpre, kpre, vtaps, ktaps, raw, bias, decay)


def inner_kernel(qpre, qtaps, keys, values, cum, cum_t, step_t, skip, queries, part):
    causal = lax.broadcasted_iota(jnp.int32, (BLOCK, BLOCK), 0) >= lax.broadcasted_iota(jnp.int32, (BLOCK, BLOCK), 1)
    low = lax.broadcasted_iota(jnp.int32, (BLOCK, LANES), 1) < 64
    for b in range(2):
        rows = slice(b * BLOCK, (b + 1) * BLOCK)
        query = convolved(qpre, qtaps, b * BLOCK, slice(0, LANES)).astype(BF16)
        queries[rows, :] = query
        scores = lax.dot_general(query, keys[rows, :], (((1,), (1,)), ((), ())), preferred_element_type=F32)
        cum_b = cum[0, rows, :]
        for pair in range(8):
            lanes = slice(pair * LANES, (pair + 1) * LANES)
            mixes = []
            for h in (2 * pair, 2 * pair + 1):
                diff = cum_b[:, h : h + 1] - cum_t[0, h : h + 1, rows]
                factor = jnp.exp(jnp.where(causal, diff, -1e30))
                mixes.append((scores * factor * step_t[0, h : h + 1, rows]).astype(BF16))
            held = values[rows, lanes]
            zero = jnp.zeros_like(held)
            split = jnp.concatenate([jnp.where(low, held, zero), jnp.where(low, zero, held)], axis=0)
            inner = jnp.dot(jnp.concatenate(mixes, axis=1), split, preferred_element_type=F32)
            part[rows, lanes] = inner + skip[:, lanes] * held.astype(F32)


def inside(qpre, qtaps, keys, values, cum, cum_t, step_t, skip):
    groups = cum.shape[0]
    rows = qpre.shape[0]
    slab_rows = rows - HALO
    wide = 1024
    col = lambda g: (0, g)
    lead = lambda g: (g, 0, 0)
    return pl.pallas_call(
        inner_kernel,
        grid=(groups,),
        in_specs=[
            pl.BlockSpec((rows, STATE), col),
            pl.BlockSpec((4, STATE), col),
            pl.BlockSpec((slab_rows, STATE), col),
            pl.BlockSpec((slab_rows, wide), col),
            pl.BlockSpec((1, slab_rows, LANES), lead),
            pl.BlockSpec((1, LANES, slab_rows), lead),
            pl.BlockSpec((1, LANES, slab_rows), lead),
            pl.BlockSpec((1, wide), col),
        ],
        out_specs=[pl.BlockSpec((slab_rows, STATE), col), pl.BlockSpec((slab_rows, wide), col)],
        out_shape=[
            jax.ShapeDtypeStruct((slab_rows, groups * STATE), BF16),
            jax.ShapeDtypeStruct((slab_rows, groups * wide), F32),
        ],
        cost_estimate=cost(groups * 1e9, groups * 4e6),
        compiler_params=pltpu.CompilerParams(vmem_limit_bytes=32 << 20),
        name="inside",
    )(qpre, qtaps, keys, values, cum, cum_t, step_t, skip)


def normed_kernel(part, flow1, flow2, flow3, local0, fall0, queries, cum, gate, gain, normed, gated):
    low = lax.broadcasted_iota(jnp.int32, (BLOCK, LANES), 1) < 64
    for b in range(2):
        rows = slice(b * BLOCK, (b + 1) * BLOCK)
        grown = jnp.exp(cum[0, rows, :])
        query = queries[rows, :]
        squares = jnp.zeros((BLOCK, LANES), F32)
        for pair in range(8):
            lanes = slice(pair * LANES, (pair + 1) * LANES)
            start = flow1[:, lanes].astype(F32) + flow2[:, lanes].astype(F32) + flow3[:, lanes].astype(F32)
            if b == 1:
                start = fall0[:, lanes] * start + local0[:, lanes]
            outer = jnp.dot(query, start.astype(BF16), preferred_element_type=F32)
            spread = pair_lanes(grown[:, 2 * pair : 2 * pair + 1], grown[:, 2 * pair + 1 : 2 * pair + 2], low)
            out = (part[rows, lanes] + spread * outer) * silu(gate[rows, lanes].astype(F32))
            gated[:, lanes] = out
            squares = squares + out * out
        scale = lax.rsqrt(jnp.sum(squares, axis=1, keepdims=True) / 1024 + 1e-5)
        for pair in range(8):
            lanes = slice(pair * LANES, (pair + 1) * LANES)
            normed[rows, lanes] = (gated[:, lanes] * scale * gain[:, lanes]).astype(BF16)


def norm(part, flows, local0, fall0, queries, cum, gate, gain):
    groups = cum.shape[0]
    slab_rows = part.shape[0]
    wide = 1024
    col = lambda g: (0, g)
    lead = lambda g: (g, 0, 0)
    return pl.pallas_call(
        normed_kernel,
        grid=(groups,),
        in_specs=[
            pl.BlockSpec((slab_rows, wide), col),
            *[pl.BlockSpec((STATE, wide), col)] * 3,
            pl.BlockSpec((STATE, wide), col),
            pl.BlockSpec((1, wide), col),
            pl.BlockSpec((slab_rows, STATE), col),
            pl.BlockSpec((1, slab_rows, LANES), lead),
            pl.BlockSpec((slab_rows, wide), col),
            pl.BlockSpec((1, wide), col),
        ],
        out_specs=pl.BlockSpec((slab_rows, wide), col),
        out_shape=jax.ShapeDtypeStruct((slab_rows, groups * wide), BF16),
        scratch_shapes=[pltpu.VMEM((BLOCK, wide), F32)],
        cost_estimate=cost(groups * 2e8, groups * 4e6),
        compiler_params=pltpu.CompilerParams(vmem_limit_bytes=32 << 20),
        name="norm",
    )(part, *flows, local0, fall0, queries, cum, gate, gain)


def out_kernel(place_ref, normed, weight, own, next1, next2, next3, edge, x):
    tp = place_ref[0]

    @pl.when(pl.program_id(0) == 0)
    def _():
        for d in range(4):
            row = pl.multiple_of((tp + d) % 4 * 64, 64)
            x[d * 64 : d * 64 + 64, :] = normed[pl.ds(row, 64), :]

    result = jnp.dot(x[...], weight[...], preferred_element_type=F32)
    own[...] = result[0:64, :]
    next1[...] = result[64:128, :].astype(BF16)
    next2[...] = result[128:192, :].astype(BF16)
    next3[...] = result[192:256, :].astype(BF16)
    edge[...] = jnp.where(tp == 0, result[192:256, :], result[64:128, :]).astype(BF16)


def project_out(place, normed, weight, first, width):
    tile = 512
    depth = weight.shape[0]
    base = first // tile
    out = pl.BlockSpec((64, tile), lambda j, _: (0, j))
    shape = lambda dtype: jax.ShapeDtypeStruct((64, width), dtype)
    return pl.pallas_call(
        out_kernel,
        grid_spec=pltpu.PrefetchScalarGridSpec(
            num_scalar_prefetch=1,
            grid=(width // tile,),
            in_specs=[
                pl.BlockSpec((256, depth), lambda j, _: (0, 0)),
                pl.BlockSpec((depth, tile), lambda j, _: (0, base + j)),
            ],
            out_specs=[out] * 5,
            scratch_shapes=[pltpu.VMEM((256, depth), BF16)],
        ),
        out_shape=[shape(F32), shape(BF16), shape(BF16), shape(BF16), shape(BF16)],
        cost_estimate=cost(512 * depth * width, 2 * depth * width),
        compiler_params=pltpu.CompilerParams(vmem_limit_bytes=32 << 20),
        name="project_out",
    )(place, normed, weight)


def added(a, b):
    return (a.astype(F32) + b.astype(F32)).astype(BF16)


def line_gather(piece):
    right1 = lax.ppermute(piece, "tp", [(0, 1), (1, 2), (2, 3)])
    left1 = lax.ppermute(piece, "tp", [(3, 2), (2, 1), (1, 0)])
    right2 = lax.ppermute(right1, "tp", [(1, 2), (2, 3)])
    left2 = lax.ppermute(left1, "tp", [(2, 1), (1, 0)])
    rot2 = right2 + left2
    last = lax.ppermute(rot2, "tp", [(2, 3), (1, 0)])
    return right1, left1, rot2, last


def line_scatter(blocks):
    own, next1, next2, next3, edge = blocks
    first = lax.ppermute(edge, "tp", [(0, 1), (3, 2)])
    middle = added(next2, first)
    right2 = lax.ppermute(middle, "tp", [(0, 1), (1, 2)])
    left2 = lax.ppermute(middle, "tp", [(3, 2), (2, 1)])
    right3 = lax.ppermute(added(next1, right2), "tp", [(0, 1), (1, 2), (2, 3)])
    left3 = lax.ppermute(added(next3, left2), "tp", [(3, 2), (2, 1), (1, 0)])
    return (own + right3.astype(F32) + left3.astype(F32)).astype(BF16)


def line_shards(
    tokens,
    gate_weight,
    value_weight,
    key_weight,
    query_weight,
    step_weight,
    value_conv,
    key_conv,
    query_conv,
    step_bias,
    decay_log,
    skip_gain,
    norm_gain,
    out_weight,
):
    width = tokens.shape[1]
    columns = gate_weight.shape[1]
    groups = columns // 1024
    depth = width // 2
    place = lax.axis_index("tp").astype(jnp.int32).reshape(1)
    gathered = [line_gather(tokens[:, c * depth : (c + 1) * depth]) for c in range(2)]
    edge_rows = tokens[56:64]
    halo = [
        lax.ppermute(edge_rows, ("ctx", "tp"), [(4 * c + 3, 4 * c + 4 + to) for c in range(3)])
        for to in range(4)
    ]
    halo = (halo[0] + halo[1]) + (halo[2] + halo[3])

    def jobs(partials, which):
        table = {
            "v": (value_weight, 512, BF16, True, False),
            "k": (key_weight, key_weight.shape[1], BF16, True, False),
            "q": (query_weight, query_weight.shape[1], BF16, True, False),
            "s": (step_weight, step_weight.shape[1], F32, True, True),
            "g": (gate_weight, 512, BF16, False, False),
        }
        made = []
        for name in which:
            weight, tile, out, has_halo, grouped = table[name]
            made.append(
                dict(
                    weight=weight,
                    tile=tile,
                    halo=has_halo,
                    out=F32 if partials is None else out,
                    grouped=grouped and partials is not None,
                    partial=None if partials is None else partials[name],
                )
            )
        return made

    inputs = [(tokens, *gathered[c], halo) for c in range(2)]
    partials = dict(zip("vkqsg", project(place, inputs[0], jobs(None, "vkqsg"), 0, depth)))
    vpre, kpre, qpre, raw = project(place, inputs[1], jobs(partials, "vkqs"), 1, depth)
    gate_in, = project(place, inputs[1], jobs(partials, "g"), 1, depth)

    def per_group(v):
        return jnp.pad(v.reshape(groups, 1, 16), ((0, 0), (0, 0), (0, LANES - 16)))

    values, keys, cum, cum_t, step_t, local0, slab, fall0, fall = states(
        vpre, kpre, value_conv, key_conv, raw, per_group(step_bias), per_group(decay_log)
    )
    flow1 = lax.ppermute(slab, "ctx", [(0, 1)])
    passed = (fall * flow1.astype(F32) + slab.astype(F32)).astype(BF16)
    flow2 = lax.ppermute(passed, "ctx", [(1, 2)])
    passed = (fall * flow2.astype(F32) + slab.astype(F32)).astype(BF16)
    flow3 = lax.ppermute(passed, "ctx", [(2, 3)])
    skip = jnp.repeat(skip_gain, 64).reshape(1, columns)
    queries, part = inside(qpre, query_conv, keys, values, cum, cum_t, step_t, skip)
    normed = norm(
        part, (flow1, flow2, flow3), local0, fall0, queries, cum, gate_in, norm_gain.reshape(1, columns)
    )
    half = width // 2
    outs = [line_scatter(project_out(place, normed, out_weight, c * half, half)) for c in range(2)]
    return jnp.concatenate(outs, axis=1)


def dispatch(*args):
    tokens, gate_weight, value_weight, key_weight, _, step_weight = args[:6]
    line = (
        lax.axis_size("tp") == 4
        and lax.axis_size("ctx") == 4
        and tokens.shape[0] == 64
        and gate_weight.shape[1] % 1024 == 0
        and key_weight.shape[1] == STATE * (gate_weight.shape[1] // 1024)
        and step_weight.shape[1] * 64 == gate_weight.shape[1]
    )
    return line_shards(*args) if line else general_shards(*args)


def solution(mesh):
    return jax.shard_map(
        dispatch,
        mesh=mesh,
        in_specs=(
            P(("groups", "ctx", "tp"), None),
            P(None, "tp"),
            P(None, "tp"),
            P(None, "tp"),
            P(None, "tp"),
            P(None, "tp"),
            P(None, "tp"),
            P(None, "tp"),
            P(None, "tp"),
            P("tp"),
            P("tp"),
            P("tp"),
            P("tp"),
            P("tp", None),
        ),
        out_specs=P(("groups", "ctx", "tp"), None),
        check_vma=False,
    )
```

```python
import functools

import jax
import jax.numpy as jnp
from jax import lax
from jax.experimental import pallas as pl
from jax.experimental.pallas import tpu as pltpu
from jax.sharding import PartitionSpec as P

STATE = 128
GROUPS = 8
INNER = 8192


def passed_along(shard, axis, by):
    count = lax.axis_size(axis)
    pairs = [(i, i + by) for i in range(count) if 0 <= i + by < count]
    return lax.ppermute(shard, axis, pairs)


def from_partner(block, axis, distance):
    count = lax.axis_size(axis)
    route = []
    for low in range(count):
        high = low | 1 << distance
        if high != low and high < count:
            route += [(low, high), (high, low)]
    return lax.ppermute(block, axis, route)


def causal_mix(padded, kernel, length):
    total = padded[0:length] * kernel[0]
    for tap_index in range(1, kernel.shape[0]):
        total = total + padded[tap_index : tap_index + length] * kernel[tap_index]
    return total


def general_shards(
    tokens,
    gate_weight,
    value_weight,
    key_weight,
    query_weight,
    step_weight,
    value_conv,
    key_conv,
    query_conv,
    step_bias,
    decay_log,
    skip_gain,
    norm_gain,
    out_weight,
):
    tok_dev = tokens.shape[0]
    slab_rows = tok_dev * lax.axis_size("tp")
    columns = gate_weight.shape[1]
    key_cols = key_weight.shape[1]
    heads_here = step_weight.shape[1]
    head_width = columns // heads_here
    block_len = min(128, slab_rows)
    block_count = slab_rows // block_len
    kernel_len = value_conv.shape[0]
    joined = jnp.concatenate(
        [gate_weight, value_weight, key_weight, query_weight, step_weight], axis=1
    )
    projected = jnp.dot(
        lax.all_gather(tokens, "tp", axis=0, tiled=True), joined, preferred_element_type=jnp.float32
    )
    gate_in = projected[:, :columns].astype(jnp.bfloat16)
    mixed_pre = projected[:, columns : 2 * columns + 2 * key_cols].astype(jnp.bfloat16)
    step_raw = projected[:, 2 * columns + 2 * key_cols :]
    border = passed_along(mixed_pre[slab_rows - (kernel_len - 1) :], "ctx", 1)
    padded = jnp.concatenate([border, mixed_pre], axis=0).astype(jnp.float32)
    kernel = jnp.concatenate([value_conv, key_conv, query_conv], axis=1)
    activated = jax.nn.silu(causal_mix(padded, kernel, slab_rows)).astype(jnp.bfloat16)
    value_act = activated[:, :columns]
    key_act = activated[:, columns : columns + key_cols]
    query_act = activated[:, columns + key_cols :]
    group_cols = max(key_cols, STATE)
    reach = group_cols // key_cols
    key_group, query_group = (key_act, query_act)
    for bit_index in range(reach.bit_length() - 1):
        other_keys, other_queries = from_partner((key_group, query_group), "tp", bit_index)
        upper = lax.axis_index("tp") // (1 << bit_index) % 2 == 1
        key_group = jnp.where(
            upper,
            jnp.concatenate([other_keys, key_group], 1),
            jnp.concatenate([key_group, other_keys], 1),
        )
        query_group = jnp.where(
            upper,
            jnp.concatenate([other_queries, query_group], 1),
            jnp.concatenate([query_group, other_queries], 1),
        )
    local_groups = group_cols // STATE
    per_group = heads_here // local_groups
    step = jax.nn.softplus(step_raw + step_bias)
    rate = -jnp.exp(decay_log) * step
    cum = jnp.cumsum(rate.reshape(block_count, block_len, heads_here), axis=1)
    step_blk = step.reshape(block_count, block_len, heads_here)
    values = value_act.reshape(block_count, block_len, heads_here, head_width)
    keys = key_group.reshape(block_count, block_len, local_groups, STATE)
    queries = query_group.reshape(block_count, block_len, local_groups, STATE)
    scores = jnp.einsum("btgn,bugn->gbtu", queries, keys, preferred_element_type=jnp.float32)
    scores = jnp.repeat(scores, per_group, axis=0)
    cum_t = jnp.transpose(cum, (2, 0, 1))
    step_t = jnp.transpose(step_blk, (2, 0, 1))
    causal = jnp.tril(jnp.ones((block_len, block_len), jnp.bool_))
    diff = cum_t[:, :, :, None] - cum_t[:, :, None, :]
    factor = jnp.where(causal, jnp.exp(jnp.where(causal, diff, 0.0)), 0.0)
    weights = (scores * factor * step_t[:, :, None, :]).astype(jnp.bfloat16)
    inner = jnp.einsum("hbtu,buhp->bthp", weights, values, preferred_element_type=jnp.float32)
    tail = jnp.exp(cum[:, -1:, :] - cum) * step_blk
    weighted = (values * tail[:, :, :, None]).astype(jnp.bfloat16)
    key_heads = jnp.repeat(keys, per_group, axis=2)
    query_heads = jnp.repeat(queries, per_group, axis=2)
    local = jnp.einsum("buhn,buhp->bhnp", key_heads, weighted, preferred_element_type=jnp.float32)
    falloff = jnp.exp(cum[:, -1, :])

    def advance(carry, item):
        fade, added = item
        return (fade[:, None, None] * carry + added, carry)

    zero_state = jnp.zeros((heads_here, STATE, head_width), jnp.float32)
    slab_state, _ = lax.scan(advance, zero_state, (falloff, local))
    slab_fall = jnp.exp(jnp.sum(cum[:, -1, :], axis=0))
    inflow = zero_state
    for turn in range(lax.axis_size("ctx") - 1):
        inflow = passed_along(
            (slab_fall[:, None, None] * inflow + slab_state).astype(jnp.bfloat16), "ctx", 1
        ).astype(jnp.float32)
    _, starts = lax.scan(advance, inflow, (falloff, local))
    outer = jnp.einsum(
        "bthn,bhnp->bthp", query_heads.astype(jnp.float32), starts, precision=lax.Precision.HIGHEST
    )
    ssm_out = (
        inner
        + jnp.exp(cum)[:, :, :, None] * outer
        + skip_gain[:, None] * values.astype(jnp.float32)
    )
    ssm_out = ssm_out.reshape(slab_rows, columns)
    gated = ssm_out * jax.nn.silu(gate_in.astype(jnp.float32))
    span = INNER // GROUPS
    piece_len = min(columns, span)
    norm_here = columns // piece_len
    squares = jnp.sum((gated * gated).reshape(slab_rows, norm_here, piece_len), axis=2)
    norm_reach = span // piece_len
    for bit_index in range(norm_reach.bit_length() - 1):
        squares = squares + from_partner(squares, "tp", bit_index)
    scale = lax.rsqrt(squares / span + 1e-05)
    normed = (gated.reshape(slab_rows, norm_here, piece_len) * scale[:, :, None]).reshape(
        slab_rows, columns
    ) * norm_gain
    normed = normed.astype(jnp.bfloat16)
    return lax.psum_scatter(
        jnp.dot(normed, out_weight, preferred_element_type=jnp.float32).astype(jnp.bfloat16),
        "tp",
        scatter_dimension=0,
        tiled=True,
    )


HALO = 16
BLOCK = 128
LANES = 128
F32 = jnp.float32
BF16 = jnp.bfloat16


def cost(flops, moved):
    return pl.CostEstimate(flops=int(flops), bytes_accessed=int(moved), transcendentals=0)


def in_hbm(array):
    return pltpu.with_memory_space_constraint(array, pltpu.HBM)


def whole(count):
    return [pl.BlockSpec(memory_space=pltpu.VMEM)] * count


def assemble(x, tp, tokens, pieces, halo, chunks, depth):
    for at, c in enumerate(chunks):
        right1, left1, rot2, last = pieces[4 * at : 4 * at + 4]
        kept = slice(c * depth, (c + 1) * depth)
        lanes = slice(at * depth, (at + 1) * depth)
        x[0:8, lanes] = jnp.zeros((8, depth), BF16)
        x[8:16, lanes] = halo[:, kept]

        def put(distance, block):
            row = pl.multiple_of(HALO + (tp + 4 - distance) % 4 * 64, 16)
            x[pl.ds(row, 64), lanes] = block

        put(0, tokens[:, kept])
        put(1, jnp.where(tp == 0, last[...], right1[...]))
        put(2, rot2[...])
        put(3, jnp.where(tp == 3, last[...], left1[...]))


def project_kernel(plan, place, tokens, halo, *refs):
    pieces, refs = refs[: 4 * len(plan["chunks"])], refs[4 * len(plan["chunks"]) :]
    jobs, depth = plan["jobs"], plan["depth"]
    weights, refs = refs[: len(jobs)], refs[len(jobs) :]
    partials = [None] * len(jobs)
    if plan["partials"]:
        partials, refs = refs[: len(jobs)], refs[len(jobs) :]
    heads = ()
    if plan["heads"]:
        heads, refs = refs[:3], refs[3:]
    outs, refs = refs[: plan["outs"]], refs[plan["outs"] :]
    x, sem, slots = refs[0], refs[1], refs[2:]
    first = plan["chunks"][0] * depth
    span = len(plan["chunks"]) * depth

    def copy(job, number, tile):
        lanes = pl.ds(tile * job["tile"], job["tile"])
        if job["kind"] == "s":
            source, target = weights[number].at[:, pl.ds(first, span)], slots[number]
        else:
            source, target = weights[number].at[pl.ds(first, span), lanes], slots[number].at[tile]
        return pltpu.make_async_copy(source, target, sem.at[job["sem"] + tile])

    for number, job in enumerate(jobs):
        for tile in range(job["tiles"]):
            copy(job, number, tile).start()
    assemble(x, place[0], tokens, pieces, halo, plan["chunks"], depth)
    for number, job in enumerate(jobs):
        out, partial, low = outs[number], partials[number], job["low"]
        if job["kind"] == "s":
            copy(job, number, 0).wait()
            result = lax.dot_general(
                x[...], slots[number][...], (((1,), (1,)), ((), ())), preferred_element_type=F32
            )
            if not plan["heads"]:
                out[...] = result
                continue
            bias, decay, skip = heads
            shifted = result + partial[...] + bias[...]
            step = jnp.maximum(shifted, 0.0) + jnp.log1p(jnp.exp(-jnp.abs(shifted)))
            rate = -jnp.exp(decay[...]) * step
            steps, rates, skips = outs[number : number + 3]
            for ref in (steps, rates, skips):
                ref[...] = jnp.zeros(ref.shape, F32)
            for group in range(steps.shape[0]):
                lanes = slice(group * 16, group * 16 + 16)
                steps[group, :, 0:16] = step[HALO:, lanes]
                rates[group, :, 0:16] = rate[HALO:, lanes]
                skips[group, 0:1, 0:16] = skip[:, lanes]
            continue

        def tile_step(tile, job=job, number=number, out=out, partial=partial, low=low):
            copy(job, number, tile).wait()
            result = jnp.dot(x[low:, :], slots[number][tile], preferred_element_type=F32)
            lanes = pl.ds(pl.multiple_of(tile * job["tile"], job["tile"]), job["tile"])
            if partial is not None:
                result = result + partial[:, lanes]
            out[:, lanes] = result.astype(out.dtype)

        if job["tiles"] == 1:
            tile_step(0)
        else:
            pl.loop(0, job["tiles"])(tile_step)


def project(place, tokens, halo, pieces, chunks, depth, weights, partials=None, heads=None):
    rows = HALO + 256
    span = len(chunks) * depth
    jobs, out_shapes, slots, sems, columns = [], [], [], 0, 0
    final = partials is not None or len(chunks) == 2
    for kind, weight in weights.items():
        width = weight.shape[0] if kind == "s" else weight.shape[1]
        tile = min(width, 512)
        low = HALO if kind == "g" else 0
        jobs.append(dict(kind=kind, tile=tile, tiles=width // tile, low=low, sem=sems))
        sems += width // tile
        columns += width
        if kind == "s":
            slots.append(pltpu.VMEM((width, span), BF16))
            groups = width // 16
            if heads is None:
                out_shapes.append(jax.ShapeDtypeStruct((rows, width), F32))
            else:
                out_shapes += [jax.ShapeDtypeStruct((groups, 256, LANES), F32)] * 2
                out_shapes.append(jax.ShapeDtypeStruct((groups, 8, LANES), F32))
        else:
            slots.append(pltpu.VMEM((width // tile, span, tile), BF16))
            out_shapes.append(jax.ShapeDtypeStruct((rows - low, width), BF16 if final else F32))
    plan = dict(
        jobs=jobs, depth=depth, chunks=chunks, partials=partials is not None, heads=heads is not None, outs=len(out_shapes)
    )
    extra = [] if partials is None else list(partials)
    extra += [] if heads is None else list(heads)
    return pl.pallas_call(
        functools.partial(project_kernel, plan),
        in_specs=[
            pl.BlockSpec(memory_space=pltpu.SMEM),
            *whole(2 + len(pieces)),
            *[pl.BlockSpec(memory_space=pltpu.HBM)] * len(weights),
            *whole(len(extra)),
        ],
        out_specs=whole(len(out_shapes)),
        out_shape=out_shapes,
        scratch_shapes=[pltpu.VMEM((rows, span), BF16), pltpu.SemaphoreType.DMA((sems,)), *slots],
        cost_estimate=cost(2 * rows * span * columns, 2 * span * columns),
        compiler_params=pltpu.CompilerParams(vmem_limit_bytes=36 << 20),
        name="project",
    )(place, tokens, halo, *pieces, *[in_hbm(w) for w in weights.values()], *extra)


def silu(v):
    return v / (1.0 + jnp.exp(-v))


def convolved(pre_ref, taps_ref, at, lanes):
    window = pre_ref[at : at + HALO + BLOCK, lanes].astype(F32)
    total = window * taps_ref[3:4, lanes]
    for back in (1, 2, 3):
        total = total + pltpu.roll(window, back, 0) * taps_ref[3 - back : 4 - back, lanes]
    return silu(total[HALO:, :])


def pair_lanes(left, right, low):
    return jnp.where(low, left, right)


def states_kernel(vpre, kpre, vtaps, ktaps, steps, rates, values, keys, cum, cum_t, step_t, local0, slab, fall0, fall):
    tri = jnp.where(
        lax.broadcasted_iota(jnp.int32, (BLOCK, BLOCK), 0) >= lax.broadcasted_iota(jnp.int32, (BLOCK, BLOCK), 1),
        1.0,
        0.0,
    )
    low = lax.broadcasted_iota(jnp.int32, (BLOCK, LANES), 1) < 64
    low1 = low[0:1, :]
    sums, tails = [], []
    for b in range(2):
        rows = slice(b * BLOCK, (b + 1) * BLOCK)
        step = steps[0, rows, :]
        total = jnp.dot(tri, rates[0, rows, :], precision=lax.Precision.HIGHEST, preferred_element_type=F32)
        cum[0, rows, :] = total
        cum_t[0, :, rows] = total.T
        step_t[0, :, rows] = step.T
        tails.append(jnp.exp(total[BLOCK - 1 :, :] - total) * step)
        sums.append(total[BLOCK - 1 :, :])
        keys[rows, :] = convolved(kpre, ktaps, b * BLOCK, slice(0, LANES)).astype(BF16)
    both = sums[0] + sums[1]
    for pair in range(8):
        lanes = slice(pair * LANES, (pair + 1) * LANES)
        kept = []
        for b in range(2):
            rows = slice(b * BLOCK, (b + 1) * BLOCK)
            act = convolved(vpre, vtaps, b * BLOCK, lanes).astype(BF16)
            values[rows, lanes] = act
            tail = pair_lanes(tails[b][:, 2 * pair : 2 * pair + 1], tails[b][:, 2 * pair + 1 : 2 * pair + 2], low)
            weighted = (act.astype(F32) * tail).astype(BF16)
            kept.append(
                lax.dot_general(keys[rows, :], weighted, (((0,), (0,)), ((), ())), preferred_element_type=F32)
            )
        spread = [
            jnp.exp(pair_lanes(s[:, 2 * pair : 2 * pair + 1], s[:, 2 * pair + 1 : 2 * pair + 2], low1))
            for s in (sums[0], sums[1], both)
        ]
        local0[:, lanes] = kept[0]
        slab[:, lanes] = (spread[1] * kept[0] + kept[1]).astype(BF16)
        fall0[:, lanes] = spread[0]
        fall[:, lanes] = spread[2]


def states(vpre, kpre, vtaps, ktaps, steps, rates):
    groups = steps.shape[0]
    rows = vpre.shape[0]
    slab_rows = rows - HALO
    wide = 1024
    col = lambda g: (0, g)
    lead = lambda g: (g, 0, 0)
    full = lambda shape, dtype: jax.ShapeDtypeStruct(shape, dtype)
    return pl.pallas_call(
        states_kernel,
        grid=(groups,),
        in_specs=[
            pl.BlockSpec((rows, wide), col),
            pl.BlockSpec((rows, STATE), col),
            pl.BlockSpec((4, wide), col),
            pl.BlockSpec((4, STATE), col),
            pl.BlockSpec((1, slab_rows, LANES), lead),
            pl.BlockSpec((1, slab_rows, LANES), lead),
        ],
        out_specs=[
            pl.BlockSpec((slab_rows, wide), col),
            pl.BlockSpec((slab_rows, STATE), col),
            pl.BlockSpec((1, slab_rows, LANES), lead),
            pl.BlockSpec((1, LANES, slab_rows), lead),
            pl.BlockSpec((1, LANES, slab_rows), lead),
            pl.BlockSpec((STATE, wide), col),
            pl.BlockSpec((STATE, wide), col),
            pl.BlockSpec((1, wide), col),
            pl.BlockSpec((1, wide), col),
        ],
        out_shape=[
            full((slab_rows, groups * wide), BF16),
            full((slab_rows, groups * STATE), BF16),
            full((groups, slab_rows, LANES), F32),
            full((groups, LANES, slab_rows), F32),
            full((groups, LANES, slab_rows), F32),
            full((STATE, groups * wide), F32),
            full((STATE, groups * wide), BF16),
            full((1, groups * wide), F32),
            full((1, groups * wide), F32),
        ],
        cost_estimate=cost(groups * 3e8, groups * 3e6),
        compiler_params=pltpu.CompilerParams(vmem_limit_bytes=32 << 20),
        name="states",
    )(vpre, kpre, vtaps, ktaps, steps, rates)


def inner_kernel(qpre, qtaps, keys, values, cum, cum_t, step_t, skip, queries, part):
    causal = lax.broadcasted_iota(jnp.int32, (BLOCK, BLOCK), 0) >= lax.broadcasted_iota(jnp.int32, (BLOCK, BLOCK), 1)
    low = lax.broadcasted_iota(jnp.int32, (BLOCK, LANES), 1) < 64
    for b in range(2):
        rows = slice(b * BLOCK, (b + 1) * BLOCK)
        query = convolved(qpre, qtaps, b * BLOCK, slice(0, LANES)).astype(BF16)
        queries[rows, :] = query
        scores = lax.dot_general(query, keys[rows, :], (((1,), (1,)), ((), ())), preferred_element_type=F32)
        cum_b = cum[0, rows, :]
        for pair in range(8):
            lanes = slice(pair * LANES, (pair + 1) * LANES)
            mixes = []
            for h in (2 * pair, 2 * pair + 1):
                diff = cum_b[:, h : h + 1] - cum_t[0, h : h + 1, rows]
                factor = jnp.exp(jnp.where(causal, diff, -1e30))
                mixes.append((scores * factor * step_t[0, h : h + 1, rows]).astype(BF16))
            held = values[rows, lanes]
            zero = jnp.zeros_like(held)
            split = jnp.concatenate([jnp.where(low, held, zero), jnp.where(low, zero, held)], axis=0)
            inner = jnp.dot(jnp.concatenate(mixes, axis=1), split, preferred_element_type=F32)
            gain = pair_lanes(skip[0, 0:1, 2 * pair : 2 * pair + 1], skip[0, 0:1, 2 * pair + 1 : 2 * pair + 2], low[0:1, :])
            part[rows, lanes] = inner + gain * held.astype(F32)


def inside(qpre, qtaps, keys, values, cum, cum_t, step_t, skip):
    groups = cum.shape[0]
    rows = qpre.shape[0]
    slab_rows = rows - HALO
    wide = 1024
    col = lambda g: (0, g)
    lead = lambda g: (g, 0, 0)
    return pl.pallas_call(
        inner_kernel,
        grid=(groups,),
        in_specs=[
            pl.BlockSpec((rows, STATE), col),
            pl.BlockSpec((4, STATE), col),
            pl.BlockSpec((slab_rows, STATE), col),
            pl.BlockSpec((slab_rows, wide), col),
            pl.BlockSpec((1, slab_rows, LANES), lead),
            pl.BlockSpec((1, LANES, slab_rows), lead),
            pl.BlockSpec((1, LANES, slab_rows), lead),
            pl.BlockSpec((1, 8, LANES), lead),
        ],
        out_specs=[pl.BlockSpec((slab_rows, STATE), col), pl.BlockSpec((slab_rows, wide), col)],
        out_shape=[
            jax.ShapeDtypeStruct((slab_rows, groups * STATE), BF16),
            jax.ShapeDtypeStruct((slab_rows, groups * wide), F32),
        ],
        cost_estimate=cost(groups * 1e9, groups * 4e6),
        compiler_params=pltpu.CompilerParams(vmem_limit_bytes=32 << 20),
        name="inside",
    )(qpre, qtaps, keys, values, cum, cum_t, step_t, skip)


def multiply_out(x, slots, copies, outs, tp, tile):
    own, next1, next2, next3, edge = outs

    @pl.loop(0, slots.shape[0])
    def _(j):
        copies(j).wait()
        result = jnp.dot(x[...], slots[j], preferred_element_type=F32)
        lanes = pl.ds(pl.multiple_of(j * tile, tile), tile)
        own[:, lanes] = result[0:64, :]
        next1[:, lanes] = result[64:128, :].astype(BF16)
        next2[:, lanes] = result[128:192, :].astype(BF16)
        next3[:, lanes] = result[192:256, :].astype(BF16)
        edge[:, lanes] = jnp.where(tp == 0, result[192:256, :], result[64:128, :]).astype(BF16)


def normed_kernel(
    first, tile, place, part, flow1, flow2, flow3, local0, fall0, queries, cum, gate, gain, weight,
    x, own, next1, next2, next3, edge, gated, slots, sem,
):
    tp = place[0]

    def copies(j):
        return pltpu.make_async_copy(weight.at[:, pl.ds(first + j * tile, tile)], slots.at[j], sem.at[j])

    for j in range(slots.shape[0]):
        copies(j).start()
    low = lax.broadcasted_iota(jnp.int32, (BLOCK, LANES), 1) < 64
    for g in range(cum.shape[0]):
        for b in range(2):
            rows = slice(b * BLOCK, (b + 1) * BLOCK)
            grown = jnp.exp(cum[g, rows, :])
            query = queries[rows, g * STATE : (g + 1) * STATE]
            squares = jnp.zeros((BLOCK, LANES), F32)
            for pair in range(8):
                lanes = slice(g * 1024 + pair * LANES, g * 1024 + (pair + 1) * LANES)
                kept = slice(pair * LANES, (pair + 1) * LANES)
                start = flow1[:, lanes].astype(F32) + flow2[:, lanes].astype(F32) + flow3[:, lanes].astype(F32)
                if b == 1:
                    start = fall0[:, lanes] * start + local0[:, lanes]
                outer = jnp.dot(query, start.astype(BF16), preferred_element_type=F32)
                spread = pair_lanes(grown[:, 2 * pair : 2 * pair + 1], grown[:, 2 * pair + 1 : 2 * pair + 2], low)
                out = (part[rows, lanes] + spread * outer) * silu(gate[rows, lanes].astype(F32))
                gated[:, kept] = out
                squares = squares + out * out
            scale = lax.rsqrt(jnp.sum(squares, axis=1, keepdims=True) / 1024 + 1e-5)
            for pair in range(8):
                lanes = slice(g * 1024 + pair * LANES, g * 1024 + (pair + 1) * LANES)
                kept = slice(pair * LANES, (pair + 1) * LANES)
                normed = (gated[:, kept] * scale * gain[:, lanes]).astype(BF16)
                for part_of in range(2):
                    row = pl.multiple_of((2 * b + part_of + 4 - tp) % 4 * 64, 64)
                    x[pl.ds(row, 64), lanes] = normed[part_of * 64 : part_of * 64 + 64, :]
    multiply_out(x, slots, copies, (own, next1, next2, next3, edge), tp, tile)


def out_shapes_of(width):
    return [jax.ShapeDtypeStruct((64, width), dtype) for dtype in (F32, BF16, BF16, BF16, BF16)]


def norm_and_out(place, part, flows, local0, fall0, queries, cum, gate, gain, weight, first, width, tile):
    rows, depth = part.shape
    return pl.pallas_call(
        functools.partial(normed_kernel, first, tile),
        in_specs=[
            pl.BlockSpec(memory_space=pltpu.SMEM),
            *whole(10),
            pl.BlockSpec(memory_space=pltpu.HBM),
        ],
        out_specs=whole(6),
        out_shape=[jax.ShapeDtypeStruct((rows, depth), BF16), *out_shapes_of(width)],
        scratch_shapes=[
            pltpu.VMEM((BLOCK, 1024), F32),
            pltpu.VMEM((width // tile, depth, tile), BF16),
            pltpu.SemaphoreType.DMA((width // tile,)),
        ],
        cost_estimate=cost(2 * rows * depth * width, 2 * depth * width),
        compiler_params=pltpu.CompilerParams(vmem_limit_bytes=36 << 20),
        name="norm_and_out",
    )(place, part, *flows, local0, fall0, queries, cum, gate, gain, in_hbm(weight))


def out_kernel(first, tile, place, x, weight, own, next1, next2, next3, edge, slots, sem):
    def copies(j):
        return pltpu.make_async_copy(weight.at[:, pl.ds(first + j * tile, tile)], slots.at[j], sem.at[j])

    for j in range(slots.shape[0]):
        copies(j).start()
    multiply_out(x, slots, copies, (own, next1, next2, next3, edge), place[0], tile)


def project_out(place, x, weight, first, width, tile):
    rows, depth = x.shape
    return pl.pallas_call(
        functools.partial(out_kernel, first, tile),
        in_specs=[pl.BlockSpec(memory_space=pltpu.SMEM), *whole(1), pl.BlockSpec(memory_space=pltpu.HBM)],
        out_specs=whole(5),
        out_shape=out_shapes_of(width),
        scratch_shapes=[
            pltpu.VMEM((width // tile, depth, tile), BF16),
            pltpu.SemaphoreType.DMA((width // tile,)),
        ],
        cost_estimate=cost(2 * rows * depth * width, 2 * depth * width),
        compiler_params=pltpu.CompilerParams(vmem_limit_bytes=36 << 20),
        name="project_out",
    )(place, x, in_hbm(weight))


def added(a, b):
    return (a.astype(F32) + b.astype(F32)).astype(BF16)


def line_gather(pieces):
    first = []
    for c, piece in enumerate(pieces):
        with jax.named_scope(f"right1_{c}"):
            right1 = lax.ppermute(piece, "tp", [(0, 1), (1, 2), (2, 3)])
        with jax.named_scope(f"left1_{c}"):
            left1 = lax.ppermute(piece, "tp", [(3, 2), (2, 1), (1, 0)])
        first.append((right1, left1))
    gathered = []
    for c, (right1, left1) in enumerate(first):
        with jax.named_scope(f"right2_{c}"):
            right2 = lax.ppermute(right1, "tp", [(1, 2), (2, 3)])
        with jax.named_scope(f"left2_{c}"):
            left2 = lax.ppermute(left1, "tp", [(2, 1), (1, 0)])
        rot2 = right2 + left2
        with jax.named_scope(f"last_{c}"):
            last = lax.ppermute(rot2, "tp", [(2, 3), (1, 0)])
        gathered.append((right1, left1, rot2, last))
    return gathered


def line_scatter(blocks, c):
    own, next1, next2, next3, edge = blocks
    with jax.named_scope(f"sum1_{c}"):
        first = lax.ppermute(edge, "tp", [(0, 1), (3, 2)])
    middle = added(next2, first)
    with jax.named_scope(f"sumright2_{c}"):
        right2 = lax.ppermute(middle, "tp", [(0, 1), (1, 2)])
    with jax.named_scope(f"sumleft2_{c}"):
        left2 = lax.ppermute(middle, "tp", [(3, 2), (2, 1)])
    with jax.named_scope(f"sumright3_{c}"):
        right3 = lax.ppermute(added(next1, right2), "tp", [(0, 1), (1, 2), (2, 3)])
    with jax.named_scope(f"sumleft3_{c}"):
        left3 = lax.ppermute(added(next3, left2), "tp", [(3, 2), (2, 1), (1, 0)])
    return (own + right3.astype(F32) + left3.astype(F32)).astype(BF16)


def line_shards(
    tokens,
    gate_weight,
    value_weight,
    key_weight,
    query_weight,
    step_weight,
    value_conv,
    key_conv,
    query_conv,
    step_bias,
    decay_log,
    skip_gain,
    norm_gain,
    out_weight,
):
    width = tokens.shape[1]
    columns = gate_weight.shape[1]
    depth = width // 2
    place = lax.axis_index("tp").astype(jnp.int32).reshape(1)
    piece0 = tokens[:, :depth]
    held, _ = lax.optimization_barrier((tokens, piece0))
    gathered = line_gather([piece0, held[:, depth:]])
    edge_rows, _ = lax.optimization_barrier((tokens[56:64], gathered[0][1]))
    halo = []
    for to in range(4):
        with jax.named_scope(f"halo{to}"):
            halo.append(
                lax.ppermute(edge_rows, ("ctx", "tp"), [(4 * c + 3, 4 * c + 4 + to) for c in range(3)])
            )
    halo = (halo[0] + halo[1]) + (halo[2] + halo[3])
    ahead = {"k": key_weight, "q": query_weight, "v": value_weight, "s": step_weight.T}
    row = lambda v: v.reshape(1, v.shape[0])
    with jax.named_scope("ahead"):
        partials = project(place, tokens, halo, gathered[0], (0,), depth, ahead)
    with jax.named_scope("behind"):
        kpre, qpre, vpre, steps, rates, skip = project(
            place, tokens, halo, gathered[1], (1,), depth, ahead, partials, (row(step_bias), row(decay_log), row(skip_gain))
        )
    with jax.named_scope("states"):
        values, keys, cum, cum_t, step_t, local0, slab, fall0, fall = states(
            vpre, kpre, value_conv, key_conv, steps, rates
        )
    with jax.named_scope("hop1"):
        flow1 = lax.ppermute(slab, "ctx", [(0, 1)])
    passed = (fall * flow1.astype(F32) + slab.astype(F32)).astype(BF16)
    with jax.named_scope("hop2"):
        flow2 = lax.ppermute(passed, "ctx", [(1, 2)])
    passed = (fall * flow2.astype(F32) + slab.astype(F32)).astype(BF16)
    with jax.named_scope("hop3"):
        flow3 = lax.ppermute(passed, "ctx", [(2, 3)])
    with jax.named_scope("inside"):
        queries, part = inside(qpre, query_conv, keys, values, cum, cum_t, step_t, skip)
    with jax.named_scope("gate"):
        (gate_in,) = project(
            place, tokens, halo, (*gathered[0], *gathered[1]), (0, 1), depth, {"g": gate_weight}
        )
    half = width // 2
    with jax.named_scope("out0"):
        x, *blocks0 = norm_and_out(
            place, part, (flow1, flow2, flow3), local0, fall0, queries, cum, gate_in, row(norm_gain), out_weight, 0, half, 512
        )
    with jax.named_scope("out1"):
        blocks1 = project_out(place, x, out_weight, half, half, 512)
    return jnp.concatenate([line_scatter(blocks0, 0), line_scatter(blocks1, 1)], axis=1)


def dispatch(*args):
    tokens, gate_weight, value_weight, key_weight, _, step_weight = args[:6]
    line = (
        lax.axis_size("tp") == 4
        and lax.axis_size("ctx") == 4
        and tokens.shape[0] == 64
        and gate_weight.shape[1] % 1024 == 0
        and key_weight.shape[1] == STATE * (gate_weight.shape[1] // 1024)
        and step_weight.shape[1] * 64 == gate_weight.shape[1]
    )
    return line_shards(*args) if line else general_shards(*args)


def solution(mesh):
    return jax.shard_map(
        dispatch,
        mesh=mesh,
        in_specs=(
            P(("groups", "ctx", "tp"), None),
            P(None, "tp"),
            P(None, "tp"),
            P(None, "tp"),
            P(None, "tp"),
            P(None, "tp"),
            P(None, "tp"),
            P(None, "tp"),
            P(None, "tp"),
            P("tp"),
            P("tp"),
            P("tp"),
            P("tp"),
            P("tp", None),
        ),
        out_specs=P(("groups", "ctx", "tp"), None),
        check_vma=False,
    )
```
